32 devices in a mesh: energy: 8 (over z, y), cell: 4 (over x, core).
Axes of the slice: x: 2, y: 2, z: 4, core: 2. Of those that a mesh axis runs over, the one named last changes fastest.
Arguments:
- retarded: bfloat16 [4, 2, 32, 256, 256], P('cell', None, 'energy'), may hold values from -0.25 to 0.25
- sigma_lesser: bfloat16 [4, 2, 32, 256, 256], P('cell', None, 'energy'), may hold values from -6 to 6
- sigma_greater: bfloat16 [4, 2, 32, 256, 256], P('cell', None, 'energy'), may hold values from -6 to 6
- coulomb: bfloat16 [4, 3, 256, 256], P('cell'), may hold values from -0.21875 to 0.21875
Outputs:
- screened: bfloat16 [4, 2, 32, 256, 256], P('cell', None, 'energy')
The draws below stay inside these ranges and needn't reach their ends.
All inputs are finite; a program needn't handle non-finite values.
Results may differ from the reference program's by a relative error of at most 0.009.
Values may be sent and summed in bfloat16 or wider, within the bound.
A program may use at most 64 MiB of HBM per device.

```python
import math
import jax
import jax.numpy as jnp
from jax import lax

NORB = 256
NE = 32
CELLS = 4


def levels(rng, shape, pieces, low, high):
    def one(position, parts):
        heights = jax.random.uniform(jax.random.fold_in(jax.random.fold_in(rng, 6), position), (parts,), jnp.float32, low / len(pieces), high / len(pieces))
        return jnp.repeat(jnp.exp(heights), shape[position] // parts).reshape((-1,) + (1,) * (len(shape) - position - 1))

    level = one(*pieces[0])
    for cut in pieces[1:]:
        level = level * one(*cut)
    return level


def noise(key, shape, width, limit, pieces=(), held_as=jnp.bfloat16):
    drawn = width * jax.random.normal(key, shape, jnp.float32)
    if pieces:
        drawn = drawn * levels(key, shape, pieces, -0.22, 0.18)
    return jnp.clip(drawn, -limit, limit).astype(held_as)


def setup_inputs(seed: int = 0) -> dict:
    keys = jax.random.split(jax.random.key(seed), 5)
    return {
        "retarded": noise(keys[0], (CELLS, 2, NE, NORB, NORB), (2 * NORB) ** -0.5, 0.25, ((0, 4), (2, 8))),
        "sigma_lesser": noise(keys[1], (CELLS, 2, NE, NORB, NORB), 1.0, 6.0, ((0, 4), (2, 8))),
        "sigma_greater": noise(keys[2], (CELLS, 2, NE, NORB, NORB), 1.0, 6.0, ((0, 4), (2, 8))),
        "coulomb": noise(keys[3], (CELLS, 3, NORB, NORB), (3 * NORB) ** -0.5, 0.21875, ((0, 4),)),
    }


def complex_product(first_re, first_im, second_re, second_im):
    first_re = first_re.astype(jnp.float32)
    first_im = first_im.astype(jnp.float32)
    second_re = second_re.astype(jnp.float32)
    second_im = second_im.astype(jnp.float32)
    real_part = jnp.einsum('eik,ekj->eij', first_re, second_re) - jnp.einsum('eik,ekj->eij', first_im, second_im)
    imag_part = jnp.einsum('eik,ekj->eij', first_re, second_im) + jnp.einsum('eik,ekj->eij', first_im, second_re)
    return (real_part.astype(jnp.bfloat16), imag_part.astype(jnp.bfloat16))

def adjoint_product(first_re, first_im, green_re, green_im):
    first_re = first_re.astype(jnp.float32)
    first_im = first_im.astype(jnp.float32)
    green_re = green_re.astype(jnp.float32)
    green_im = green_im.astype(jnp.float32)
    real_part = jnp.einsum('eik,ejk->eij', first_re, green_re) + jnp.einsum('eik,ejk->eij', first_im, green_im)
    imag_part = jnp.einsum('eik,ejk->eij', first_im, green_re) - jnp.einsum('eik,ejk->eij', first_re, green_im)
    return jnp.stack([real_part, imag_part]).astype(jnp.bfloat16)

def triple(green, sigma):
    half_re, half_im = complex_product(green[0], green[1], sigma[0], sigma[1])
    return adjoint_product(half_re, half_im, green[0], green[1])

def tables(energies):
    length = 2 * energies
    frequency = lax.broadcasted_iota(jnp.int32, (length, energies), 0)
    energy_index = lax.broadcasted_iota(jnp.int32, (length, energies), 1)
    angles = 2.0 * math.pi / length * (frequency * energy_index % length).astype(jnp.float32)
    cos_table = jnp.cos(angles)
    sin_table = jnp.sin(angles)
    forward_first = jnp.concatenate([jnp.concatenate([cos_table, sin_table], 1), jnp.concatenate([-sin_table, cos_table], 1)], 0)
    forward_second = jnp.concatenate([jnp.concatenate([cos_table, -sin_table], 1), jnp.concatenate([sin_table, cos_table], 1)], 0)
    factor = 1.0 / (length * math.sqrt(energies))
    inverse = jnp.concatenate([jnp.concatenate([cos_table.T, -sin_table.T], 1), jnp.concatenate([sin_table.T, cos_table.T], 1)], 0) * factor
    return (forward_first.astype(jnp.bfloat16), forward_second.astype(jnp.bfloat16), inverse.astype(jnp.bfloat16))

def correlate(lesser, mirrored):
    energies = lesser.shape[1]
    length = 2 * energies
    elements = lesser.shape[2] * lesser.shape[3]
    forward_first, forward_second, inverse = tables(energies)
    first_flat = lesser.reshape(2 * energies, elements)
    second_flat = mirrored.reshape(2 * energies, elements)
    spec_first = jnp.dot(forward_first, first_flat, preferred_element_type=jnp.float32)
    spec_second = jnp.dot(forward_second, second_flat, preferred_element_type=jnp.float32)
    left_re, left_im = (spec_first[:length], spec_first[length:])
    right_re, right_im = (spec_second[:length], spec_second[length:])
    product = jnp.concatenate([left_re * right_re - left_im * right_im, left_re * right_im + left_im * right_re], 0).astype(jnp.bfloat16)
    lag_values = jnp.dot(inverse, product, preferred_element_type=jnp.float32)
    return lag_values.reshape(lesser.shape).astype(jnp.bfloat16)

def reference(retarded, sigma_lesser, sigma_greater, coulomb):
    polarized = []
    for cell_index in range(CELLS):
        lesser = triple(retarded[cell_index], sigma_lesser[cell_index])
        greater = triple(retarded[cell_index], sigma_greater[cell_index])
        polarized.append(correlate(lesser, jnp.swapaxes(greater, -1, -2)))
    outputs = []
    for cell_index in range(CELLS):
        summed = jnp.zeros((2, NE, NORB, NORB), jnp.float32)
        for offset in (-1, 0, 1):
            neighbour = cell_index + offset
            if 0 <= neighbour < CELLS:
                weights = coulomb[cell_index, offset + 1].astype(jnp.float32)
                summed = summed + jnp.einsum('ik,cekj->ceij', weights, polarized[neighbour].astype(jnp.float32))
        outputs.append(summed.astype(jnp.bfloat16))
    return jnp.stack(outputs)
```

```python
import functools
import math

import jax
import jax.numpy as jnp
from jax import lax
from jax.experimental import pallas as pl
from jax.experimental.pallas import tpu as pltpu
from jax.sharding import PartitionSpec as P

MESH = pl.DeviceIdType.MESH
ROWS = 16
LANES = 128
F32 = jnp.float32
BF16 = jnp.bfloat16


def nn(a, b):
    return jnp.dot(a, b, preferred_element_type=F32)


def nt(a, b):
    return lax.dot_general(a, b, (((1,), (1,)), ((), ())), preferred_element_type=F32)


def fused_kernel(
    n, cells, green, sig_l, sig_g, coulomb, out,
    send, recv, send_p, pol, total,
    send_sem, recv_sem, ret_send_sem, ret_recv_sem, halo_send_sem, halo_recv_sem,
):
    me = lax.axis_index("energy")
    cell = lax.axis_index("cell")
    local = green.shape[1]
    norb = green.shape[2]
    strip = norb // n
    row_parts, col_parts = strip // ROWS, norb // LANES
    chunks = row_parts * col_parts
    has_low = cell > 0
    has_high = cell < cells - 1

    barrier = pltpu.get_barrier_semaphore()

    @pl.loop(1, n)
    def _(k):
        pl.semaphore_signal(barrier, inc=1, device_id={"energy": lax.rem(me + k, n)}, device_id_type=MESH)

    @pl.when(has_low)
    def _():
        pl.semaphore_signal(barrier, inc=1, device_id={"cell": cell - 1}, device_id_type=MESH)

    @pl.when(has_high)
    def _():
        pl.semaphore_signal(barrier, inc=1, device_id={"cell": cell + 1}, device_id_type=MESH)

    def put(value, comp, e):
        value = value.astype(BF16).reshape(n, strip, norb)
        for q in range(chunks):
            r, c = divmod(q, col_parts)
            send[q, :, comp, e] = value[:, r * ROWS:(r + 1) * ROWS, c * LANES:(c + 1) * LANES]

    @pl.loop(0, local)
    def _(e):
        g_re, g_im = green[0, e], green[1, e]
        l_re, l_im = sig_l[0, e], sig_l[1, e]
        half_re = (nn(g_re, l_re) - nn(g_im, l_im)).astype(BF16)
        half_im = (nn(g_re, l_im) + nn(g_im, l_re)).astype(BF16)
        put(nt(half_re, g_re) + nt(half_im, g_im), 0, e)
        put(nt(half_im, g_re) - nt(half_re, g_im), 1, e)
        s_re, s_im = sig_g[0, e], sig_g[1, e]
        half_re = (nn(g_re, s_re) - nn(g_im, s_im)).astype(BF16)
        half_im = (nn(g_re, s_im) + nn(g_im, s_re)).astype(BF16)
        put(nt(g_re, half_re) + nt(g_im, half_im), 2, e)
        put(nt(g_re, half_im) - nt(g_im, half_re), 3, e)

    pl.semaphore_wait(barrier, n - 1 + has_low.astype(jnp.int32) + has_high.astype(jnp.int32))

    def strip_copy(q, slot, peer):
        return pltpu.make_async_remote_copy(
            src_ref=send.at[q, peer], dst_ref=recv.at[q, slot],
            send_sem=send_sem.at[q, peer], recv_sem=recv_sem.at[q, slot],
            device_id={"energy": peer}, device_id_type=MESH,
        )

    @pl.loop(0, chunks)
    def _(q):
        @pl.loop(1, n)
        def _(k):
            strip_copy(q, me, lax.rem(me + k, n)).start()

    @pl.loop(0, chunks)
    def _(q):
        recv[q, me] = send[q, me]
        recv[q, n] = jnp.zeros_like(recv[q, n])

    @pl.when(jnp.logical_not(has_low))
    def _():
        pol[0] = jnp.zeros_like(pol[0])

    @pl.when(jnp.logical_not(has_high))
    def _():
        pol[2] = jnp.zeros_like(pol[2])

    def window(slot, owner, q):
        rows = pl.ds(pl.multiple_of(q // col_parts * ROWS, ROWS), ROWS)
        cols = pl.ds(pl.multiple_of(q % col_parts * LANES, LANES), LANES)
        return pol.at[slot, :, :, owner, rows, cols]

    def return_copy(q, slot, peer):
        return pltpu.make_async_remote_copy(
            src_ref=send_p.at[q, peer], dst_ref=window(1, slot, q),
            send_sem=ret_send_sem.at[q, peer], recv_sem=ret_recv_sem.at[q, slot],
            device_id={"energy": peer}, device_id_type=MESH,
        )

    factor = 1.0 / math.sqrt(n * local)

    def correlate(q, b):
        def step(a, acc):
            first = [
                (recv[q, a + b + i // local, 0, i % local].astype(F32), recv[q, a + b + i // local, 1, i % local].astype(F32))
                for i in range(2 * local - 1)
            ]
            acc = list(acc)
            for e in range(local):
                x_re, x_im = recv[q, a, 2, e].astype(F32), recv[q, a, 3, e].astype(F32)
                for w in range(local):
                    y_re, y_im = first[e + w]
                    acc[2 * w] = acc[2 * w] + (y_re * x_re - y_im * x_im)
                    acc[2 * w + 1] = acc[2 * w + 1] + (y_re * x_im + y_im * x_re)
            return tuple(acc)

        zero = jnp.zeros((ROWS, LANES), F32)
        acc = lax.fori_loop(0, n - b, step, (zero,) * (2 * local))
        for w in range(local):
            send_p[q, b, 0, w] = (acc[2 * w] * factor).astype(BF16)
            send_p[q, b, 1, w] = (acc[2 * w + 1] * factor).astype(BF16)

    @pl.loop(0, chunks)
    def _(q):
        @pl.loop(1, n)
        def _(k):
            strip_copy(q, lax.rem(me + k, n), lax.rem(me + k, n)).wait_recv()

        @pl.loop(1, n)
        def _(k):
            peer = lax.rem(me + k, n)
            correlate(q, peer)
            return_copy(q, me, peer).start()

        correlate(q, me)
        window(1, me, q)[...] = send_p[q, me]

    def halo_copy(q, slot, other):
        rows = pl.ds(pl.multiple_of(q // col_parts * ROWS, ROWS), ROWS)
        cols = pl.ds(pl.multiple_of(q % col_parts * LANES, LANES), LANES)
        return pltpu.make_async_remote_copy(
            src_ref=pol.at[1, :, :, :, rows, cols], dst_ref=pol.at[slot, :, :, :, rows, cols],
            send_sem=halo_send_sem.at[q, slot // 2], recv_sem=halo_recv_sem.at[q, slot // 2],
            device_id={"cell": other}, device_id_type=MESH,
        )

    @pl.loop(0, chunks)
    def _(q):
        @pl.loop(1, n)
        def _(k):
            return_copy(q, lax.rem(me + k, n), lax.rem(me + k, n)).wait_recv()

        @pl.when(has_low)
        def _():
            halo_copy(q, 2, cell - 1).start()

        @pl.when(has_high)
        def _():
            halo_copy(q, 0, cell + 1).start()

    def polarized(slot, c, e):
        return pol[slot, c, e].reshape(norb, norb)

    @pl.loop(0, local)
    def _(e):
        for c in range(2):
            total[c, e] = nn(coulomb[1], polarized(1, c, e))

    @pl.loop(0, chunks)
    def _(q):
        @pl.when(has_low)
        def _():
            halo_copy(q, 0, cell - 1).wait_recv()
            halo_copy(q, 2, cell - 1).wait_send()

        @pl.when(has_high)
        def _():
            halo_copy(q, 2, cell + 1).wait_recv()
            halo_copy(q, 0, cell + 1).wait_send()

    @pl.loop(0, local)
    def _(e):
        for c in range(2):
            summed = total[c, e] + nn(coulomb[0], polarized(0, c, e)) + nn(coulomb[2], polarized(2, c, e))
            out[c, e] = summed.astype(BF16)

    @pl.loop(0, chunks)
    def _(q):
        @pl.loop(1, n)
        def _(k):
            peer = lax.rem(me + k, n)
            strip_copy(q, me, peer).wait_send()
            return_copy(q, me, peer).wait_send()


def fused(n, cells, retarded, sigma_lesser, sigma_greater, coulomb):
    green = retarded[0]
    local, norb = green.shape[1], green.shape[2]
    strip = norb // n
    chunks = strip // ROWS * (norb // LANES)
    vmem = pl.BlockSpec(memory_space=pltpu.VMEM)
    dma = pltpu.SemaphoreType.DMA
    result = pl.pallas_call(
        functools.partial(fused_kernel, n, cells),
        out_shape=jax.ShapeDtypeStruct(green.shape, BF16),
        in_specs=[vmem] * 4,
        out_specs=vmem,
        scratch_shapes=[
            pltpu.VMEM((chunks, n, 4, local, ROWS, LANES), BF16),
            pltpu.VMEM((chunks, n + 1, 4, local, ROWS, LANES), BF16),
            pltpu.VMEM((chunks, n, 2, local, ROWS, LANES), BF16),
            pltpu.VMEM((3, 2, local, n, strip, norb), BF16),
            pltpu.VMEM((2, local, norb, norb), F32),
            dma((chunks, n)), dma((chunks, n)), dma((chunks, n)), dma((chunks, n)),
            dma((chunks, 2)), dma((chunks, 2)),
        ],
        compiler_params=pltpu.CompilerParams(
            collective_id=0, has_side_effects=True, vmem_limit_bytes=48 * 1024 * 1024
        ),
    )(green, sigma_lesser[0], sigma_greater[0], coulomb[0])
    return result[None]


def thin(n, cells, retarded, sigma_lesser, sigma_greater, coulomb):
    green = retarded[0]
    local = green.shape[1]

    def halves(sigma):
        def product(x, y):
            return jnp.einsum("eik,ekj->eij", x, y, preferred_element_type=F32)

        re = product(green[0], sigma[0]) - product(green[1], sigma[1])
        im = product(green[0], sigma[1]) + product(green[1], sigma[0])
        return re.astype(BF16), im.astype(BF16)

    def adjoint(x, y):
        return jnp.einsum("eik,ejk->eij", x, y, preferred_element_type=F32)

    re, im = halves(sigma_lesser[0])
    lesser = jnp.stack([adjoint(re, green[0]) + adjoint(im, green[1]), adjoint(im, green[0]) - adjoint(re, green[1])])
    re, im = halves(sigma_greater[0])
    greater = jnp.stack([adjoint(green[0], re) + adjoint(green[1], im), adjoint(green[0], im) - adjoint(green[1], re)])
    first = lax.all_to_all(lesser.astype(BF16), "energy", split_axis=2, concat_axis=1, tiled=True).astype(F32)
    second = lax.all_to_all(greater.astype(BF16), "energy", split_axis=2, concat_axis=1, tiled=True).astype(F32)
    energies = n * local
    padded = jnp.concatenate([first, jnp.zeros_like(first)], axis=1)

    def lag(w):
        y = lax.dynamic_slice_in_dim(padded, w, energies, axis=1)
        re = jnp.sum(y[0] * second[0] - y[1] * second[1], axis=0)
        im = jnp.sum(y[0] * second[1] + y[1] * second[0], axis=0)
        return (jnp.stack([re, im]) / math.sqrt(energies)).astype(BF16)

    polarized = jnp.swapaxes(lax.map(lag, jnp.arange(energies)), 0, 1)
    polarized = lax.all_to_all(polarized, "energy", split_axis=1, concat_axis=2, tiled=True)
    up = [(i, i + 1) for i in range(cells - 1)]
    low = lax.ppermute(polarized, "cell", up)
    high = lax.ppermute(polarized, "cell", [(t, s) for s, t in up])
    stacked = jnp.stack([low, polarized, high])
    summed = jnp.einsum("dik,dcekj->ceij", coulomb[0], stacked, preferred_element_type=F32)
    return summed.astype(BF16)[None]


def solution(mesh):
    n, cells = mesh.shape["energy"], mesh.shape["cell"]

    def on_device(retarded, sigma_lesser, sigma_greater, coulomb):
        norb = retarded.shape[-1]
        whole_tiles = norb % LANES == 0 and norb % (n * ROWS) == 0
        plan = fused if whole_tiles else thin
        return plan(n, cells, retarded, sigma_lesser, sigma_greater, coulomb)

    in_specs = (
        P("cell", None, "energy", None, None),
        P("cell", None, "energy", None, None),
        P("cell", None, "energy", None, None),
        P("cell", None, None, None),
    )
    out_specs = P("cell", None, "energy", None, None)
    return jax.shard_map(
        on_device, mesh=mesh, in_specs=in_specs, out_specs=out_specs, check_vma=False
    )
```

```python
import functools
import math

import jax
import jax.numpy as jnp
from jax import lax
from jax.experimental import pallas as pl
from jax.experimental.pallas import tpu as pltpu
from jax.sharding import PartitionSpec as P

MESH = pl.DeviceIdType.MESH
ROWS = 16
LANES = 128
QUARTERS = 4
DELAY = 4
F32 = jnp.float32
BF16 = jnp.bfloat16


def nn(a, b):
    return jnp.dot(a, b, preferred_element_type=F32)


def nt(a, b):
    return lax.dot_general(a, b, (((1,), (1,)), ((), ())), preferred_element_type=F32)


def fused_kernel(
    n, cells, green, sig_l, sig_g, coulomb, out,
    send, recv, part, send_p, pol, total,
    send_sem, recv_sem, relay_send_sem, relay_recv_sem, part_send_sem, part_recv_sem,
    ret_send_sem, ret_recv_sem, halo_send_sem, halo_recv_sem,
):
    me = lax.axis_index("energy")
    cell = lax.axis_index("cell")
    local = green.shape[1]
    norb = green.shape[2]
    width = n // QUARTERS
    half = 2 * width
    quarter, place = me // width, lax.rem(me, width)
    home = jnp.where(me < half, 1, 2)
    strip = norb // width
    col_parts = norb // LANES
    chunks = strip // ROWS * col_parts
    has_low = cell > 0
    has_high = cell < cells - 1

    barrier = pltpu.get_barrier_semaphore()

    @pl.loop(1, n)
    def _(k):
        pl.semaphore_signal(barrier, inc=1, device_id={"energy": lax.rem(me + k, n)}, device_id_type=MESH)

    @pl.when(has_low)
    def _():
        pl.semaphore_signal(barrier, inc=1, device_id={"cell": cell - 1}, device_id_type=MESH)

    @pl.when(has_high)
    def _():
        pl.semaphore_signal(barrier, inc=1, device_id={"cell": cell + 1}, device_id_type=MESH)

    def put(value, comp, e):
        value = value.astype(BF16).reshape(width, strip, norb)
        for q in range(chunks):
            r, c = divmod(q, col_parts)
            send[q, :, comp, e] = value[:, r * ROWS:(r + 1) * ROWS, c * LANES:(c + 1) * LANES]

    @pl.loop(0, local)
    def _(e):
        g_re, g_im = green[0, e], green[1, e]
        l_re, l_im = sig_l[0, e], sig_l[1, e]
        half_re = (nn(g_re, l_re) - nn(g_im, l_im)).astype(BF16)
        half_im = (nn(g_re, l_im) + nn(g_im, l_re)).astype(BF16)
        put(nt(half_re, g_re) + nt(half_im, g_im), 0, e)
        put(nt(half_im, g_re) - nt(half_re, g_im), 1, e)
        s_re, s_im = sig_g[0, e], sig_g[1, e]
        half_re = (nn(g_re, s_re) - nn(g_im, s_im)).astype(BF16)
        half_im = (nn(g_re, s_im) + nn(g_im, s_re)).astype(BF16)
        put(nt(g_re, half_re) + nt(g_im, half_im), 2, e)
        put(nt(g_re, half_im) - nt(g_im, half_re), 3, e)

    pl.semaphore_wait(barrier, n - 1 + has_low.astype(jnp.int32) + has_high.astype(jnp.int32))


    def strip_copy(q, slot, where):
        return pltpu.make_async_remote_copy(
            src_ref=send.at[q, where], dst_ref=recv.at[q, slot],
            send_sem=send_sem.at[q, where], recv_sem=recv_sem.at[q, slot],
            device_id={"energy": home * width + where}, device_id_type=MESH,
        )

    def each_target(act):
        for where in range(width):
            pl.when(home * width + where != me)(functools.partial(act, where))

    @pl.loop(0, chunks)
    def _(q):
        each_target(lambda where: strip_copy(q, me, where).start())

    @pl.when(quarter == home)
    def _():
        @pl.loop(0, chunks)
        def _(q):
            recv[q, me] = send[q, place]

    blank = jnp.zeros((2, local, ROWS, LANES), BF16)

    @pl.when(quarter == 1)
    def _():
        @pl.loop(0, chunks)
        def _(q):
            recv[q, half, 0:2] = blank

    @pl.when(quarter == 2)
    def _():
        @pl.loop(0, chunks)
        def _(q):
            recv[q, half - 1, 0:2] = blank
            recv[q, n, 0:2] = blank

    @pl.when(jnp.logical_not(has_low))
    def _():
        pol[0] = jnp.zeros_like(pol[0])

    @pl.when(jnp.logical_not(has_high))
    def _():
        pol[2] = jnp.zeros_like(pol[2])

    def spot(q):
        rows = pl.ds(pl.multiple_of(q // col_parts * ROWS, ROWS), ROWS)
        return rows, pl.ds(pl.multiple_of(q % col_parts * LANES, LANES), LANES)

    def relay_copy(q):
        return pltpu.make_async_remote_copy(
            src_ref=recv.at[q, 0:half, 2:4], dst_ref=recv.at[q, 0:half, 2:4],
            send_sem=relay_send_sem.at[q], recv_sem=relay_recv_sem.at[q],
            device_id={"energy": 2 * width + place}, device_id_type=MESH,
        )

    def part_copy(q):
        return pltpu.make_async_remote_copy(
            src_ref=send_p.at[q, 0:half], dst_ref=part.at[q],
            send_sem=part_send_sem.at[q], recv_sem=part_recv_sem.at[q],
            device_id={"energy": width + place}, device_id_type=MESH,
        )

    def return_copy(q, where, owner):
        return pltpu.make_async_remote_copy(
            src_ref=send_p.at[q, owner], dst_ref=pol.at[1, :, :, where, *spot(q)],
            send_sem=ret_send_sem.at[q, owner], recv_sem=ret_recv_sem.at[q, where],
            device_id={"energy": owner}, device_id_type=MESH,
        )

    def halo_copy(q, slot, other):
        return pltpu.make_async_remote_copy(
            src_ref=pol.at[1, :, :, :, *spot(q)], dst_ref=pol.at[slot, :, :, :, *spot(q)],
            send_sem=halo_send_sem.at[q, slot // 2], recv_sem=halo_recv_sem.at[q, slot // 2],
            device_id={"cell": other}, device_id_type=MESH,
        )

    factor = 1.0 / math.sqrt(n * local)

    def correlate(q, b, first_step, last_step):
        def step(a, acc):
            first = [
                (recv[q, a + b + i // local, 0, i % local].astype(F32), recv[q, a + b + i // local, 1, i % local].astype(F32))
                for i in range(2 * local - 1)
            ]
            acc = list(acc)
            for e in range(local):
                x_re, x_im = recv[q, a, 2, e].astype(F32), recv[q, a, 3, e].astype(F32)
                for w in range(local):
                    y_re, y_im = first[e + w]
                    acc[2 * w] = acc[2 * w] + (y_re * x_re - y_im * x_im)
                    acc[2 * w + 1] = acc[2 * w + 1] + (y_re * x_im + y_im * x_re)
            return tuple(acc)

        zero = jnp.zeros((ROWS, LANES), F32)
        acc = lax.fori_loop(first_step, last_step, step, (zero,) * (2 * local))
        return [value * factor for value in acc]

    def hand_out(q, owner):
        @pl.when(owner != me)
        def _():
            return_copy(q, place, owner).start()

        @pl.when(owner == me)
        def _():
            pol[1, :, :, place, *spot(q)] = send_p[q, owner]

    def gather(q):
        for slot in range(n):
            belongs = (quarter == 1) if slot < half else (quarter == 2)

            @pl.when(jnp.logical_and(belongs, me != slot))
            def _():
                strip_copy(q, slot, 0).wait_recv()

    def halo(q):
        for where in range(width):
            @pl.when(home * width + where != me)
            def _():
                return_copy(q, where, 0).wait_recv()

        @pl.when(has_low)
        def _():
            halo_copy(q, 2, cell - 1).start()

        @pl.when(has_high)
        def _():
            halo_copy(q, 0, cell + 1).start()

    @pl.when(quarter == 2)
    def _():
        @pl.loop(0, chunks)
        def _(q):
            gather(q)
            relay_copy(q).wait_recv()

            @pl.loop(0, n)
            def _(b):
                acc = correlate(q, b, jnp.maximum(half - 1 - b, 0), n - b)
                for w in range(local):
                    send_p[q, b, 0, w] = acc[2 * w].astype(BF16)
                    send_p[q, b, 1, w] = acc[2 * w + 1].astype(BF16)

                @pl.when(b == half)
                def _():
                    part_copy(q).start()

                @pl.when(b >= half)
                def _():
                    hand_out(q, b)

            @pl.when(q > 0)
            def _():
                halo(q - 1)

        halo(chunks - 1)

    delay = min(DELAY, chunks)

    @pl.when(quarter == 1)
    def _():
        @pl.loop(0, chunks + delay + 1)
        def _(t):
            @pl.when(t < chunks)
            def _():
                gather(t)
                relay_copy(t).start()

            @pl.when(jnp.logical_and(t >= delay, t < chunks + delay))
            def _():
                q = t - delay
                part_copy(q).wait_recv()

                @pl.loop(0, half)
                def _(b):
                    acc = correlate(q, b, 0, half - b)
                    for w in range(local):
                        send_p[q, b, 0, w] = (acc[2 * w] + part[q, b, 0, w].astype(F32)).astype(BF16)
                        send_p[q, b, 1, w] = (acc[2 * w + 1] + part[q, b, 1, w].astype(F32)).astype(BF16)
                    hand_out(q, b)

            @pl.when(t > delay)
            def _():
                halo(t - delay - 1)

    @pl.when(quarter != home)
    def _():
        @pl.loop(0, chunks)
        def _(q):
            halo(q)

    def polarized(slot, c, e):
        return pol[slot, c, e].reshape(norb, norb)

    @pl.loop(0, local)
    def _(e):
        for c in range(2):
            total[c, e] = nn(coulomb[1], polarized(1, c, e))

    @pl.loop(0, chunks)
    def _(q):
        @pl.when(has_low)
        def _():
            halo_copy(q, 0, cell - 1).wait_recv()
            halo_copy(q, 2, cell - 1).wait_send()

        @pl.when(has_high)
        def _():
            halo_copy(q, 2, cell + 1).wait_recv()
            halo_copy(q, 0, cell + 1).wait_send()

    @pl.loop(0, local)
    def _(e):
        for c in range(2):
            summed = total[c, e] + nn(coulomb[0], polarized(0, c, e)) + nn(coulomb[2], polarized(2, c, e))
            out[c, e] = summed.astype(BF16)

    @pl.loop(0, chunks)
    def _(q):
        each_target(lambda where: strip_copy(q, me, where).wait_send())

        @pl.when(quarter == 1)
        def _():
            relay_copy(q).wait_send()

        @pl.when(quarter == 2)
        def _():
            part_copy(q).wait_send()

        @pl.when(quarter == home)
        def _():
            @pl.loop(0, half)
            def _(b):
                owner = (home - 1) * half + b

                @pl.when(owner != me)
                def _():
                    return_copy(q, place, owner).wait_send()


def fused(n, cells, retarded, sigma_lesser, sigma_greater, coulomb):
    green = retarded[0]
    local, norb = green.shape[1], green.shape[2]
    width = n // QUARTERS
    half = 2 * width
    strip = norb // width
    chunks = strip // ROWS * (norb // LANES)
    vmem = pl.BlockSpec(memory_space=pltpu.VMEM)
    dma = pltpu.SemaphoreType.DMA
    result = pl.pallas_call(
        functools.partial(fused_kernel, n, cells),
        out_shape=jax.ShapeDtypeStruct(green.shape, BF16),
        in_specs=[vmem] * 4,
        out_specs=vmem,
        scratch_shapes=[
            pltpu.VMEM((chunks, width, 4, local, ROWS, LANES), BF16),
            pltpu.VMEM((chunks, n + 1, 4, local, ROWS, LANES), BF16),
            pltpu.VMEM((chunks, half, 2, local, ROWS, LANES), BF16),
            pltpu.VMEM((chunks, n, 2, local, ROWS, LANES), BF16),
            pltpu.VMEM((3, 2, local, width, strip, norb), BF16),
            pltpu.VMEM((2, local, norb, norb), F32),
            dma((chunks, width)), dma((chunks, n)),
            dma((chunks,)), dma((chunks,)), dma((chunks,)), dma((chunks,)),
            dma((chunks, n)), dma((chunks, width)),
            dma((chunks, 2)), dma((chunks, 2)),
        ],
        compiler_params=pltpu.CompilerParams(
            collective_id=0, has_side_effects=True, vmem_limit_bytes=56 * 1024 * 1024
        ),
    )(green, sigma_lesser[0], sigma_greater[0], coulomb[0])
    return result[None]


def thin(n, cells, retarded, sigma_lesser, sigma_greater, coulomb):
    green = retarded[0]
    local = green.shape[1]

    def halves(sigma):
        def product(x, y):
            return jnp.einsum("eik,ekj->eij", x, y, preferred_element_type=F32)

        re = product(green[0], sigma[0]) - product(green[1], sigma[1])
        im = product(green[0], sigma[1]) + product(green[1], sigma[0])
        return re.astype(BF16), im.astype(BF16)

    def adjoint(x, y):
        return jnp.einsum("eik,ejk->eij", x, y, preferred_element_type=F32)

    re, im = halves(sigma_lesser[0])
    lesser = jnp.stack([adjoint(re, green[0]) + adjoint(im, green[1]), adjoint(im, green[0]) - adjoint(re, green[1])])
    re, im = halves(sigma_greater[0])
    greater = jnp.stack([adjoint(green[0], re) + adjoint(green[1], im), adjoint(green[0], im) - adjoint(green[1], re)])
    first = lax.all_to_all(lesser.astype(BF16), "energy", split_axis=2, concat_axis=1, tiled=True).astype(F32)
    second = lax.all_to_all(greater.astype(BF16), "energy", split_axis=2, concat_axis=1, tiled=True).astype(F32)
    energies = n * local
    padded = jnp.concatenate([first, jnp.zeros_like(first)], axis=1)

    def lag(w):
        y = lax.dynamic_slice_in_dim(padded, w, energies, axis=1)
        re = jnp.sum(y[0] * second[0] - y[1] * second[1], axis=0)
        im = jnp.sum(y[0] * second[1] + y[1] * second[0], axis=0)
        return (jnp.stack([re, im]) / math.sqrt(energies)).astype(BF16)

    polarized = jnp.swapaxes(lax.map(lag, jnp.arange(energies)), 0, 1)
    polarized = lax.all_to_all(polarized, "energy", split_axis=1, concat_axis=2, tiled=True)
    up = [(i, i + 1) for i in range(cells - 1)]
    low = lax.ppermute(polarized, "cell", up)
    high = lax.ppermute(polarized, "cell", [(t, s) for s, t in up])
    stacked = jnp.stack([low, polarized, high])
    summed = jnp.einsum("dik,dcekj->ceij", coulomb[0], stacked, preferred_element_type=F32)
    return summed.astype(BF16)[None]


def solution(mesh):
    n, cells = mesh.shape["energy"], mesh.shape["cell"]

    def on_device(retarded, sigma_lesser, sigma_greater, coulomb):
        norb = retarded.shape[-1]
        whole_tiles = n % QUARTERS == 0 and norb % LANES == 0 and norb % (n // QUARTERS * ROWS) == 0
        plan = fused if whole_tiles else thin
        return plan(n, cells, retarded, sigma_lesser, sigma_greater, coulomb)

    in_specs = (
        P("cell", None, "energy", None, None),
        P("cell", None, "energy", None, None),
        P("cell", None, "energy", None, None),
        P("cell", None, None, None),
    )
    out_specs = P("cell", None, "energy", None, None)
    return jax.shard_map(
        on_device, mesh=mesh, in_specs=in_specs, out_specs=out_specs, check_vma=False
    )
```

```python
import functools
import math

import jax
import jax.numpy as jnp
from jax import lax
from jax.experimental import pallas as pl
from jax.experimental.pallas import tpu as pltpu
from jax.sharding import PartitionSpec as P

MESH = pl.DeviceIdType.MESH
ROWS = 16
LANES = 128
QUARTERS = 4
DELAY = 6
LATE = 4
LEAD = 3
F32 = jnp.float32
BF16 = jnp.bfloat16


def nn(a, b):
    return jnp.dot(a, b, preferred_element_type=F32)


def nt(a, b):
    return lax.dot_general(a, b, (((1,), (1,)), ((), ())), preferred_element_type=F32)


def fused_kernel(
    n, cells, green_in, sig_l_in, sig_g_in, coulomb_in, out,
    green, sig_l, sig_g, coulomb, in_sem, coulomb_sem, send, recv, part, send_p, pol, total,
    send_sem, recv_sem, forward_send_sem, forward_recv_sem, relay_send_sem, relay_recv_sem, part_send_sem, part_recv_sem,
    ret_send_sem, ret_recv_sem, halo_send_sem, halo_recv_sem,
):
    me = lax.axis_index("energy")
    cell = lax.axis_index("cell")
    local = green.shape[1]
    norb = green.shape[2]
    width = n // QUARTERS
    half = 2 * width
    quarter, place = me // width, lax.rem(me, width)
    home = jnp.where(me < half, 1, 2)
    strip = norb // width
    col_parts = norb // LANES
    chunks = strip // ROWS * col_parts
    has_low = cell > 0
    has_high = cell < cells - 1

    def loads(e):
        return [
            pltpu.make_async_copy(source.at[:, e], held.at[:, e], in_sem.at[i, e])
            for i, (source, held) in enumerate(((green_in, green), (sig_l_in, sig_l), (sig_g_in, sig_g)))
        ]

    for e in range(local):
        for load in loads(e):
            load.start()
    coulomb_load = pltpu.make_async_copy(coulomb_in, coulomb, coulomb_sem)
    coulomb_load.start()

    barrier = pltpu.get_barrier_semaphore()

    @pl.loop(1, n)
    def _(k):
        pl.semaphore_signal(barrier, inc=1, device_id={"energy": lax.rem(me + k, n)}, device_id_type=MESH)

    @pl.when(has_low)
    def _():
        pl.semaphore_signal(barrier, inc=1, device_id={"cell": cell - 1}, device_id_type=MESH)

    @pl.when(has_high)
    def _():
        pl.semaphore_signal(barrier, inc=1, device_id={"cell": cell + 1}, device_id_type=MESH)

    def put(value, comp, e):
        value = value.astype(BF16).reshape(width, strip, norb)
        for q in range(chunks):
            r, c = divmod(q, col_parts)
            send[q, :, comp, e] = value[:, r * ROWS:(r + 1) * ROWS, c * LANES:(c + 1) * LANES]

    @pl.loop(0, local)
    def _(e):
        for load in loads(e):
            load.wait()
        g_re, g_im = green[0, e], green[1, e]
        l_re, l_im = sig_l[0, e], sig_l[1, e]
        half_re = (nn(g_re, l_re) - nn(g_im, l_im)).astype(BF16)
        half_im = (nn(g_re, l_im) + nn(g_im, l_re)).astype(BF16)
        put(nt(half_re, g_re) + nt(half_im, g_im), 0, e)
        put(nt(half_im, g_re) - nt(half_re, g_im), 1, e)
        s_re, s_im = sig_g[0, e], sig_g[1, e]
        half_re = (nn(g_re, s_re) - nn(g_im, s_im)).astype(BF16)
        half_im = (nn(g_re, s_im) + nn(g_im, s_re)).astype(BF16)
        put(nt(g_re, half_re) + nt(g_im, half_im), 2, e)
        put(nt(g_re, half_im) - nt(g_im, half_re), 3, e)

    pl.semaphore_wait(barrier, n - 1 + has_low.astype(jnp.int32) + has_high.astype(jnp.int32))


    def strip_copy(q, slot, where):
        return pltpu.make_async_remote_copy(
            src_ref=send.at[q, where], dst_ref=recv.at[q, slot],
            send_sem=send_sem.at[q, where], recv_sem=recv_sem.at[q, slot],
            device_id={"energy": quarter * width + where}, device_id_type=MESH,
        )

    def each_target(act):
        for where in range(width):
            pl.when(where != place)(functools.partial(act, where))

    lead = jnp.where(quarter == home, min(LEAD, chunks), chunks)

    @pl.loop(0, lead)
    def _(q):
        each_target(lambda where: strip_copy(q, me, where).start())

    def more(q):
        @pl.when(q + lead < chunks)
        def _():
            each_target(lambda where: strip_copy(q + lead, me, where).start())

    @pl.loop(0, chunks)
    def _(q):
        recv[q, me] = send[q, place]

    blank = jnp.zeros((2, local, ROWS, LANES), BF16)

    @pl.when(quarter == 1)
    def _():
        @pl.loop(0, chunks)
        def _(q):
            recv[q, half, 0:2] = blank

    @pl.when(quarter == 2)
    def _():
        @pl.loop(0, chunks)
        def _(q):
            recv[q, half - 1, 0:2] = blank
            recv[q, n, 0:2] = blank

    @pl.when(jnp.logical_not(has_low))
    def _():
        pol[0] = jnp.zeros_like(pol[0])

    @pl.when(jnp.logical_not(has_high))
    def _():
        pol[2] = jnp.zeros_like(pol[2])

    def spot(q):
        rows = pl.ds(pl.multiple_of(q // col_parts * ROWS, ROWS), ROWS)
        return rows, pl.ds(pl.multiple_of(q % col_parts * LANES, LANES), LANES)

    def forward_copy(q, kind):
        block = (q, pl.ds(quarter * width, width), slice(2 * kind, 2 * kind + 2))
        return pltpu.make_async_remote_copy(
            src_ref=recv.at[block], dst_ref=recv.at[block],
            send_sem=forward_send_sem.at[q, kind], recv_sem=forward_recv_sem.at[q, kind],
            device_id={"energy": home * width + place}, device_id_type=MESH,
        )

    def relay_copy(q):
        return pltpu.make_async_remote_copy(
            src_ref=recv.at[q, 0:half, 2:4], dst_ref=recv.at[q, 0:half, 2:4],
            send_sem=relay_send_sem.at[q], recv_sem=relay_recv_sem.at[q],
            device_id={"energy": 2 * width + place}, device_id_type=MESH,
        )

    def part_copy(q):
        return pltpu.make_async_remote_copy(
            src_ref=send_p.at[q, 0:half], dst_ref=part.at[q],
            send_sem=part_send_sem.at[q], recv_sem=part_recv_sem.at[q],
            device_id={"energy": width + place}, device_id_type=MESH,
        )

    def return_copy(q, where, owner):
        return pltpu.make_async_remote_copy(
            src_ref=send_p.at[q, owner], dst_ref=pol.at[1, :, :, where, *spot(q)],
            send_sem=ret_send_sem.at[q, owner], recv_sem=ret_recv_sem.at[q, where],
            device_id={"energy": owner}, device_id_type=MESH,
        )

    def halo_copy(q, slot, other):
        return pltpu.make_async_remote_copy(
            src_ref=pol.at[1, :, :, :, *spot(q)], dst_ref=pol.at[slot, :, :, :, *spot(q)],
            send_sem=halo_send_sem.at[q, slot // 2], recv_sem=halo_recv_sem.at[q, slot // 2],
            device_id={"cell": other}, device_id_type=MESH,
        )

    factor = 1.0 / math.sqrt(n * local)

    def correlate(q, b, first_step, last_step):
        def step(a, acc):
            first = [
                (recv[q, a + b + i // local, 0, i % local].astype(F32), recv[q, a + b + i // local, 1, i % local].astype(F32))
                for i in range(2 * local - 1)
            ]
            acc = list(acc)
            for e in range(local):
                x_re, x_im = recv[q, a, 2, e].astype(F32), recv[q, a, 3, e].astype(F32)
                for w in range(local):
                    y_re, y_im = first[e + w]
                    acc[2 * w] = acc[2 * w] + (y_re * x_re - y_im * x_im)
                    acc[2 * w + 1] = acc[2 * w + 1] + (y_re * x_im + y_im * x_re)
            return tuple(acc)

        zero = jnp.zeros((ROWS, LANES), F32)
        acc = lax.fori_loop(first_step, last_step, step, (zero,) * (2 * local))
        return [value * factor for value in acc]

    def hand_out(q, owner):
        @pl.when(owner != me)
        def _():
            return_copy(q, place, owner).start()

        @pl.when(owner == me)
        def _():
            pol[1, :, :, place, *spot(q)] = send_p[q, owner]

    def gather(q):
        each_target(lambda where: strip_copy(q, quarter * width + where, where).wait_recv())

    def halo(q):
        for where in range(width):
            @pl.when(home * width + where != me)
            def _():
                return_copy(q, where, 0).wait_recv()

        @pl.when(has_low)
        def _():
            halo_copy(q, 2, cell - 1).start()

        @pl.when(has_high)
        def _():
            halo_copy(q, 0, cell + 1).start()

    @pl.when(quarter == 2)
    def _():
        @pl.loop(0, chunks)
        def _(q):
            gather(q)
            more(q)
            forward_copy(q, 1).wait_recv()
            forward_copy(q, 0).wait_recv()
            relay_copy(q).wait_recv()

            @pl.loop(0, n)
            def _(b):
                acc = correlate(q, b, jnp.maximum(half - 1 - b, 0), n - b)
                for w in range(local):
                    send_p[q, b, 0, w] = acc[2 * w].astype(BF16)
                    send_p[q, b, 1, w] = acc[2 * w + 1].astype(BF16)

                @pl.when(b == half)
                def _():
                    part_copy(q).start()

                @pl.when(b >= half)
                def _():
                    hand_out(q, b)

            @pl.when(q >= LATE)
            def _():
                halo(q - LATE)

        for q in range(max(chunks - LATE, 0), chunks):
            halo(q)

    delay = min(DELAY, chunks)

    @pl.when(quarter == 1)
    def _():
        @pl.loop(0, chunks + delay + LATE)
        def _(t):
            @pl.when(t < chunks)
            def _():
                gather(t)
                forward_copy(t, 1).wait_recv()
                relay_copy(t).start()
                more(t)

            @pl.when(jnp.logical_and(t >= delay, t < chunks + delay))
            def _():
                q = t - delay
                forward_copy(q, 0).wait_recv()
                part_copy(q).wait_recv()

                @pl.loop(0, half)
                def _(b):
                    acc = correlate(q, b, 0, half - b)
                    for w in range(local):
                        send_p[q, b, 0, w] = (acc[2 * w] + part[q, b, 0, w].astype(F32)).astype(BF16)
                        send_p[q, b, 1, w] = (acc[2 * w + 1] + part[q, b, 1, w].astype(F32)).astype(BF16)
                    hand_out(q, b)

            @pl.when(t >= delay + LATE)
            def _():
                halo(t - delay - LATE)

    @pl.when(quarter != home)
    def _():
        @pl.loop(0, chunks)
        def _(q):
            gather(q)
            forward_copy(q, 1).start()
            forward_copy(q, 0).start()

        @pl.loop(0, chunks)
        def _(q):
            halo(q)

    def polarized(slot, c, e):
        return pol[slot, c, e].reshape(norb, norb)

    coulomb_load.wait()

    @pl.loop(0, local)
    def _(e):
        for c in range(2):
            total[c, e] = nn(coulomb[1], polarized(1, c, e))

    @pl.loop(0, chunks)
    def _(q):
        @pl.when(has_low)
        def _():
            halo_copy(q, 0, cell - 1).wait_recv()
            halo_copy(q, 2, cell - 1).wait_send()

        @pl.when(has_high)
        def _():
            halo_copy(q, 2, cell + 1).wait_recv()
            halo_copy(q, 0, cell + 1).wait_send()

    @pl.loop(0, local)
    def _(e):
        for c in range(2):
            summed = total[c, e] + nn(coulomb[0], polarized(0, c, e)) + nn(coulomb[2], polarized(2, c, e))
            out[c, e] = summed.astype(BF16)

    @pl.loop(0, chunks)
    def _(q):
        each_target(lambda where: strip_copy(q, me, where).wait_send())

        @pl.when(quarter != home)
        def _():
            forward_copy(q, 1).wait_send()
            forward_copy(q, 0).wait_send()

        @pl.when(quarter == 1)
        def _():
            relay_copy(q).wait_send()

        @pl.when(quarter == 2)
        def _():
            part_copy(q).wait_send()

        @pl.when(quarter == home)
        def _():
            @pl.loop(0, half)
            def _(b):
                owner = (home - 1) * half + b

                @pl.when(owner != me)
                def _():
                    return_copy(q, place, owner).wait_send()


def fused(n, cells, retarded, sigma_lesser, sigma_greater, coulomb):
    green = retarded[0]
    local, norb = green.shape[1], green.shape[2]
    width = n // QUARTERS
    half = 2 * width
    strip = norb // width
    chunks = strip // ROWS * (norb // LANES)
    vmem = pl.BlockSpec(memory_space=pltpu.VMEM)
    dma = pltpu.SemaphoreType.DMA
    result = pl.pallas_call(
        functools.partial(fused_kernel, n, cells),
        out_shape=jax.ShapeDtypeStruct(green.shape, BF16),
        in_specs=[pl.BlockSpec(memory_space=pltpu.HBM)] * 4,
        out_specs=vmem,
        scratch_shapes=[
            pltpu.VMEM(green.shape, BF16),
            pltpu.VMEM(green.shape, BF16),
            pltpu.VMEM(green.shape, BF16),
            pltpu.VMEM(coulomb.shape[1:], BF16),
            dma((3, local)), dma,
            pltpu.VMEM((chunks, width, 4, local, ROWS, LANES), BF16),
            pltpu.VMEM((chunks, n + 1, 4, local, ROWS, LANES), BF16),
            pltpu.VMEM((chunks, half, 2, local, ROWS, LANES), BF16),
            pltpu.VMEM((chunks, n, 2, local, ROWS, LANES), BF16),
            pltpu.VMEM((3, 2, local, width, strip, norb), BF16),
            pltpu.VMEM((2, local, norb, norb), F32),
            dma((chunks, width)), dma((chunks, n)), dma((chunks, 2)), dma((chunks, 2)),
            dma((chunks,)), dma((chunks,)), dma((chunks,)), dma((chunks,)),
            dma((chunks, n)), dma((chunks, width)),
            dma((chunks, 2)), dma((chunks, 2)),
        ],
        compiler_params=pltpu.CompilerParams(
            collective_id=0, has_side_effects=True, vmem_limit_bytes=56 * 1024 * 1024
        ),
    )(green, sigma_lesser[0], sigma_greater[0], coulomb[0])
    return result[None]


def thin(n, cells, retarded, sigma_lesser, sigma_greater, coulomb):
    green = retarded[0]
    local = green.shape[1]

    def halves(sigma):
        def product(x, y):
            return jnp.einsum("eik,ekj->eij", x, y, preferred_element_type=F32)

        re = product(green[0], sigma[0]) - product(green[1], sigma[1])
        im = product(green[0], sigma[1]) + product(green[1], sigma[0])
        return re.astype(BF16), im.astype(BF16)

    def adjoint(x, y):
        return jnp.einsum("eik,ejk->eij", x, y, preferred_element_type=F32)

    re, im = halves(sigma_lesser[0])
    lesser = jnp.stack([adjoint(re, green[0]) + adjoint(im, green[1]), adjoint(im, green[0]) - adjoint(re, green[1])])
    re, im = halves(sigma_greater[0])
    greater = jnp.stack([adjoint(green[0], re) + adjoint(green[1], im), adjoint(green[0], im) - adjoint(green[1], re)])
    first = lax.all_to_all(lesser.astype(BF16), "energy", split_axis=2, concat_axis=1, tiled=True).astype(F32)
    second = lax.all_to_all(greater.astype(BF16), "energy", split_axis=2, concat_axis=1, tiled=True).astype(F32)
    energies = n * local
    padded = jnp.concatenate([first, jnp.zeros_like(first)], axis=1)

    def lag(w):
        y = lax.dynamic_slice_in_dim(padded, w, energies, axis=1)
        re = jnp.sum(y[0] * second[0] - y[1] * second[1], axis=0)
        im = jnp.sum(y[0] * second[1] + y[1] * second[0], axis=0)
        return (jnp.stack([re, im]) / math.sqrt(energies)).astype(BF16)

    polarized = jnp.swapaxes(lax.map(lag, jnp.arange(energies)), 0, 1)
    polarized = lax.all_to_all(polarized, "energy", split_axis=1, concat_axis=2, tiled=True)
    up = [(i, i + 1) for i in range(cells - 1)]
    low = lax.ppermute(polarized, "cell", up)
    high = lax.ppermute(polarized, "cell", [(t, s) for s, t in up])
    stacked = jnp.stack([low, polarized, high])
    summed = jnp.einsum("dik,dcekj->ceij", coulomb[0], stacked, preferred_element_type=F32)
    return summed.astype(BF16)[None]


def solution(mesh):
    n, cells = mesh.shape["energy"], mesh.shape["cell"]

    def on_device(retarded, sigma_lesser, sigma_greater, coulomb):
        norb = retarded.shape[-1]
        whole_tiles = n % QUARTERS == 0 and norb % LANES == 0 and norb % (n // QUARTERS * ROWS) == 0
        plan = fused if whole_tiles else thin
        return plan(n, cells, retarded, sigma_lesser, sigma_greater, coulomb)

    in_specs = (
        P("cell", None, "energy", None, None),
        P("cell", None, "energy", None, None),
        P("cell", None, "energy", None, None),
        P("cell", None, None, None),
    )
    out_specs = P("cell", None, "energy", None, None)
    return jax.shard_map(
        on_device, mesh=mesh, in_specs=in_specs, out_specs=out_specs, check_vma=False
    )
```

```python
import functools
import math

import jax
import jax.numpy as jnp
from jax import lax
from jax.experimental import pallas as pl
from jax.experimental.pallas import tpu as pltpu
from jax.sharding import PartitionSpec as P

MESH = pl.DeviceIdType.MESH
ROWS = 16
LANES = 128
QUARTERS = 4
DELAY = 6
LATE = 4
LAG = 0
SHIFT = 4
LEAD = 3
F32 = jnp.float32
BF16 = jnp.bfloat16


def nn(a, b):
    return jnp.dot(a, b, preferred_element_type=F32)


def nt(a, b):
    return lax.dot_general(a, b, (((1,), (1,)), ((), ())), preferred_element_type=F32)


def fused_kernel(
    n, cells, green_in, sig_l_in, sig_g_in, coulomb_in, out,
    green, sig_l, sig_g, coulomb, in_sem, coulomb_sem, send, recv, part, send_p, pol, total,
    send_sem, recv_sem, forward_send_sem, forward_recv_sem, relay_send_sem, relay_recv_sem, part_send_sem, part_recv_sem,
    ret_send_sem, ret_recv_sem, halo_send_sem, halo_recv_sem,
):
    me = lax.axis_index("energy")
    cell = lax.axis_index("cell")
    local = green.shape[1]
    norb = green.shape[2]
    width = n // QUARTERS
    half = 2 * width
    quarter, place = me // width, lax.rem(me, width)
    home = jnp.where(me < half, 1, 2)
    strip = norb // width
    col_parts = norb // LANES
    chunks = strip // ROWS * col_parts
    has_low = cell > 0
    has_high = cell < cells - 1

    def loads(e):
        return [
            pltpu.make_async_copy(source.at[:, e], held.at[:, e], in_sem.at[i, e])
            for i, (source, held) in enumerate(((green_in, green), (sig_l_in, sig_l), (sig_g_in, sig_g)))
        ]

    for e in range(local):
        for load in loads(e):
            load.start()
    coulomb_load = pltpu.make_async_copy(coulomb_in, coulomb, coulomb_sem)
    coulomb_load.start()

    barrier = pltpu.get_barrier_semaphore()

    @pl.loop(1, n)
    def _(k):
        pl.semaphore_signal(barrier, inc=1, device_id={"energy": lax.rem(me + k, n)}, device_id_type=MESH)

    @pl.when(has_low)
    def _():
        pl.semaphore_signal(barrier, inc=1, device_id={"cell": cell - 1}, device_id_type=MESH)

    @pl.when(has_high)
    def _():
        pl.semaphore_signal(barrier, inc=1, device_id={"cell": cell + 1}, device_id_type=MESH)

    def put(value, comp, e):
        value = value.astype(BF16).reshape(width, strip, norb)
        for q in range(chunks):
            r, c = divmod(q, col_parts)
            send[q, :, comp, e] = value[:, r * ROWS:(r + 1) * ROWS, c * LANES:(c + 1) * LANES]

    @pl.loop(0, local)
    def _(e):
        for load in loads(e):
            load.wait()
        g_re, g_im = green[0, e], green[1, e]
        l_re, l_im = sig_l[0, e], sig_l[1, e]
        half_re = (nn(g_re, l_re) - nn(g_im, l_im)).astype(BF16)
        half_im = (nn(g_re, l_im) + nn(g_im, l_re)).astype(BF16)
        put(nt(half_re, g_re) + nt(half_im, g_im), 0, e)
        put(nt(half_im, g_re) - nt(half_re, g_im), 1, e)
        s_re, s_im = sig_g[0, e], sig_g[1, e]
        half_re = (nn(g_re, s_re) - nn(g_im, s_im)).astype(BF16)
        half_im = (nn(g_re, s_im) + nn(g_im, s_re)).astype(BF16)
        put(nt(g_re, half_re) + nt(g_im, half_im), 2, e)
        put(nt(g_re, half_im) - nt(g_im, half_re), 3, e)

    pl.semaphore_wait(barrier, n - 1 + has_low.astype(jnp.int32) + has_high.astype(jnp.int32))


    def strip_copy(q, slot, where):
        return pltpu.make_async_remote_copy(
            src_ref=send.at[q, where], dst_ref=recv.at[q, slot],
            send_sem=send_sem.at[q, where], recv_sem=recv_sem.at[q, slot],
            device_id={"energy": quarter * width + where}, device_id_type=MESH,
        )

    def each_target(act):
        for where in range(width):
            pl.when(where != place)(functools.partial(act, where))

    lead = jnp.where(quarter == home, min(LEAD, chunks), chunks)

    @pl.loop(0, lead)
    def _(q):
        each_target(lambda where: strip_copy(q, me, where).start())

    def more(q):
        @pl.when(q + lead < chunks)
        def _():
            each_target(lambda where: strip_copy(q + lead, me, where).start())

    @pl.loop(0, chunks)
    def _(q):
        recv[q, me] = send[q, place]

    blank = jnp.zeros((2, local, ROWS, LANES), BF16)

    @pl.when(quarter == 1)
    def _():
        @pl.loop(0, chunks)
        def _(q):
            recv[q, half, 0:2] = blank

    @pl.when(quarter == 2)
    def _():
        @pl.loop(0, chunks)
        def _(q):
            recv[q, half - 1, 0:2] = blank
            recv[q, n, 0:2] = blank

    @pl.when(jnp.logical_not(has_low))
    def _():
        pol[0] = jnp.zeros_like(pol[0])

    @pl.when(jnp.logical_not(has_high))
    def _():
        pol[2] = jnp.zeros_like(pol[2])

    def spot(q):
        rows = pl.ds(pl.multiple_of(q // col_parts * ROWS, ROWS), ROWS)
        return rows, pl.ds(pl.multiple_of(q % col_parts * LANES, LANES), LANES)

    def forward_copy(q, kind):
        block = (q, pl.ds(quarter * width, width), slice(2 * kind, 2 * kind + 2))
        return pltpu.make_async_remote_copy(
            src_ref=recv.at[block], dst_ref=recv.at[block],
            send_sem=forward_send_sem.at[q, kind], recv_sem=forward_recv_sem.at[q, kind],
            device_id={"energy": home * width + place}, device_id_type=MESH,
        )

    def relay_copy(q, origin):
        block = (q, slice(origin * width, (origin + 1) * width), slice(2, 4))
        return pltpu.make_async_remote_copy(
            src_ref=recv.at[block], dst_ref=recv.at[block],
            send_sem=relay_send_sem.at[q, origin], recv_sem=relay_recv_sem.at[q, origin],
            device_id={"energy": 2 * width + place}, device_id_type=MESH,
        )

    def part_copy(q):
        return pltpu.make_async_remote_copy(
            src_ref=send_p.at[q, 0:half], dst_ref=part.at[q],
            send_sem=part_send_sem.at[q], recv_sem=part_recv_sem.at[q],
            device_id={"energy": width + place}, device_id_type=MESH,
        )

    def return_copy(q, where, owner):
        return pltpu.make_async_remote_copy(
            src_ref=send_p.at[q, owner], dst_ref=pol.at[1, :, :, where, *spot(q)],
            send_sem=ret_send_sem.at[q, owner], recv_sem=ret_recv_sem.at[q, where],
            device_id={"energy": owner}, device_id_type=MESH,
        )

    def halo_copy(q, slot, other):
        return pltpu.make_async_remote_copy(
            src_ref=pol.at[1, :, :, :, *spot(q)], dst_ref=pol.at[slot, :, :, :, *spot(q)],
            send_sem=halo_send_sem.at[q, slot // 2], recv_sem=halo_recv_sem.at[q, slot // 2],
            device_id={"cell": other}, device_id_type=MESH,
        )

    factor = 1.0 / math.sqrt(n * local)

    def correlate(q, b, first_step, last_step):
        def step(a, acc):
            first = [
                (recv[q, a + b + i // local, 0, i % local].astype(F32), recv[q, a + b + i // local, 1, i % local].astype(F32))
                for i in range(2 * local - 1)
            ]
            acc = list(acc)
            for e in range(local):
                x_re, x_im = recv[q, a, 2, e].astype(F32), recv[q, a, 3, e].astype(F32)
                for w in range(local):
                    y_re, y_im = first[e + w]
                    acc[2 * w] = acc[2 * w] + (y_re * x_re - y_im * x_im)
                    acc[2 * w + 1] = acc[2 * w + 1] + (y_re * x_im + y_im * x_re)
            return tuple(acc)

        zero = jnp.zeros((ROWS, LANES), F32)
        acc = lax.fori_loop(first_step, last_step, step, (zero,) * (2 * local))
        return [value * factor for value in acc]

    def hand_out(q, owner):
        @pl.when(owner != me)
        def _():
            return_copy(q, place, owner).start()

        @pl.when(owner == me)
        def _():
            pol[1, :, :, place, *spot(q)] = send_p[q, owner]

    def gather(q):
        each_target(lambda where: strip_copy(q, quarter * width + where, where).wait_recv())

    def halo(q):
        for where in range(width):
            @pl.when(home * width + where != me)
            def _():
                return_copy(q, where, 0).wait_recv()

        @pl.when(has_low)
        def _():
            halo_copy(q, 2, cell - 1).start()

        @pl.when(has_high)
        def _():
            halo_copy(q, 0, cell + 1).start()

    @pl.when(quarter == 2)
    def _():
        @pl.loop(0, chunks)
        def _(q):
            gather(q)
            more(q)
            forward_copy(q, 1).wait_recv()
            forward_copy(q, 0).wait_recv()
            relay_copy(q, 1).wait_recv()
            relay_copy(q, 0).wait_recv()

            @pl.loop(0, n)
            def _(b):
                acc = correlate(q, b, jnp.maximum(half - 1 - b, 0), n - b)
                for w in range(local):
                    send_p[q, b, 0, w] = acc[2 * w].astype(BF16)
                    send_p[q, b, 1, w] = acc[2 * w + 1].astype(BF16)

                @pl.when(b == half)
                def _():
                    part_copy(q).start()

                @pl.when(b >= half)
                def _():
                    hand_out(q, b)

            @pl.when(q >= LATE)
            def _():
                halo(q - LATE)

        for q in range(max(chunks - LATE, 0), chunks):
            halo(q)

    delay = min(DELAY, chunks)
    lag = min(LAG, delay)

    @pl.when(quarter == 1)
    def _():
        @pl.loop(0, chunks + delay + LATE)
        def _(t):
            @pl.when(t < chunks)
            def _():
                gather(t)
                relay_copy(t, 1).start()
                more(t)

            @pl.when(jnp.logical_and(t >= lag, t < chunks + lag))
            def _():
                forward_copy(t - lag, 1).wait_recv()
                relay_copy(t - lag, 0).start()

            @pl.when(jnp.logical_and(t >= delay, t < chunks + delay))
            def _():
                q = t - delay
                forward_copy(q, 0).wait_recv()
                part_copy(q).wait_recv()

                @pl.loop(0, half)
                def _(b):
                    acc = correlate(q, b, 0, half - b)
                    for w in range(local):
                        send_p[q, b, 0, w] = (acc[2 * w] + part[q, b, 0, w].astype(F32)).astype(BF16)
                        send_p[q, b, 1, w] = (acc[2 * w + 1] + part[q, b, 1, w].astype(F32)).astype(BF16)
                    hand_out(q, b)

            @pl.when(t >= delay + LATE)
            def _():
                halo(t - delay - LATE)

    @pl.when(quarter != home)
    def _():
        shift = jnp.where(quarter == 0, min(SHIFT, chunks), 0)

        @pl.loop(0, chunks + shift)
        def _(q):
            @pl.when(q < chunks)
            def _():
                gather(q)
                forward_copy(q, 1).start()

            @pl.when(q >= shift)
            def _():
                forward_copy(q - shift, 0).start()

        @pl.loop(0, chunks)
        def _(q):
            halo(q)

    def polarized(slot, c, e):
        return pol[slot, c, e].reshape(norb, norb)

    coulomb_load.wait()

    @pl.loop(0, local)
    def _(e):
        for c in range(2):
            total[c, e] = nn(coulomb[1], polarized(1, c, e))

    @pl.loop(0, chunks)
    def _(q):
        @pl.when(has_low)
        def _():
            halo_copy(q, 0, cell - 1).wait_recv()
            halo_copy(q, 2, cell - 1).wait_send()

        @pl.when(has_high)
        def _():
            halo_copy(q, 2, cell + 1).wait_recv()
            halo_copy(q, 0, cell + 1).wait_send()

    @pl.loop(0, local)
    def _(e):
        for c in range(2):
            summed = total[c, e] + nn(coulomb[0], polarized(0, c, e)) + nn(coulomb[2], polarized(2, c, e))
            out[c, e] = summed.astype(BF16)

    @pl.loop(0, chunks)
    def _(q):
        each_target(lambda where: strip_copy(q, me, where).wait_send())

        @pl.when(quarter != home)
        def _():
            forward_copy(q, 1).wait_send()
            forward_copy(q, 0).wait_send()

        @pl.when(quarter == 1)
        def _():
            relay_copy(q, 0).wait_send()
            relay_copy(q, 1).wait_send()

        @pl.when(quarter == 2)
        def _():
            part_copy(q).wait_send()

        @pl.when(quarter == home)
        def _():
            @pl.loop(0, half)
            def _(b):
                owner = (home - 1) * half + b

                @pl.when(owner != me)
                def _():
                    return_copy(q, place, owner).wait_send()


def fused(n, cells, retarded, sigma_lesser, sigma_greater, coulomb):
    green = retarded[0]
    local, norb = green.shape[1], green.shape[2]
    width = n // QUARTERS
    half = 2 * width
    strip = norb // width
    chunks = strip // ROWS * (norb // LANES)
    vmem = pl.BlockSpec(memory_space=pltpu.VMEM)
    dma = pltpu.SemaphoreType.DMA
    result = pl.pallas_call(
        functools.partial(fused_kernel, n, cells),
        out_shape=jax.ShapeDtypeStruct(green.shape, BF16),
        in_specs=[pl.BlockSpec(memory_space=pltpu.HBM)] * 4,
        out_specs=vmem,
        scratch_shapes=[
            pltpu.VMEM(green.shape, BF16),
            pltpu.VMEM(green.shape, BF16),
            pltpu.VMEM(green.shape, BF16),
            pltpu.VMEM(coulomb.shape[1:], BF16),
            dma((3, local)), dma,
            pltpu.VMEM((chunks, width, 4, local, ROWS, LANES), BF16),
            pltpu.VMEM((chunks, n + 1, 4, local, ROWS, LANES), BF16),
            pltpu.VMEM((chunks, half, 2, local, ROWS, LANES), BF16),
            pltpu.VMEM((chunks, n, 2, local, ROWS, LANES), BF16),
            pltpu.VMEM((3, 2, local, width, strip, norb), BF16),
            pltpu.VMEM((2, local, norb, norb), F32),
            dma((chunks, width)), dma((chunks, n)), dma((chunks, 2)), dma((chunks, 2)),
            dma((chunks, 2)), dma((chunks, 2)), dma((chunks,)), dma((chunks,)),
            dma((chunks, n)), dma((chunks, width)),
            dma((chunks, 2)), dma((chunks, 2)),
        ],
        compiler_params=pltpu.CompilerParams(
            collective_id=0, has_side_effects=True, vmem_limit_bytes=56 * 1024 * 1024
        ),
    )(green, sigma_lesser[0], sigma_greater[0], coulomb[0])
    return result[None]


def thin(n, cells, retarded, sigma_lesser, sigma_greater, coulomb):
    green = retarded[0]
    local = green.shape[1]

    def halves(sigma):
        def product(x, y):
            return jnp.einsum("eik,ekj->eij", x, y, preferred_element_type=F32)

        re = product(green[0], sigma[0]) - product(green[1], sigma[1])
        im = product(green[0], sigma[1]) + product(green[1], sigma[0])
        return re.astype(BF16), im.astype(BF16)

    def adjoint(x, y):
        return jnp.einsum("eik,ejk->eij", x, y, preferred_element_type=F32)

    re, im = halves(sigma_lesser[0])
    lesser = jnp.stack([adjoint(re, green[0]) + adjoint(im, green[1]), adjoint(im, green[0]) - adjoint(re, green[1])])
    re, im = halves(sigma_greater[0])
    greater = jnp.stack([adjoint(green[0], re) + adjoint(green[1], im), adjoint(green[0], im) - adjoint(green[1], re)])
    first = lax.all_to_all(lesser.astype(BF16), "energy", split_axis=2, concat_axis=1, tiled=True).astype(F32)
    second = lax.all_to_all(greater.astype(BF16), "energy", split_axis=2, concat_axis=1, tiled=True).astype(F32)
    energies = n * local
    padded = jnp.concatenate([first, jnp.zeros_like(first)], axis=1)

    def lag(w):
        y = lax.dynamic_slice_in_dim(padded, w, energies, axis=1)
        re = jnp.sum(y[0] * second[0] - y[1] * second[1], axis=0)
        im = jnp.sum(y[0] * second[1] + y[1] * second[0], axis=0)
        return (jnp.stack([re, im]) / math.sqrt(energies)).astype(BF16)

    polarized = jnp.swapaxes(lax.map(lag, jnp.arange(energies)), 0, 1)
    polarized = lax.all_to_all(polarized, "energy", split_axis=1, concat_axis=2, tiled=True)
    up = [(i, i + 1) for i in range(cells - 1)]
    low = lax.ppermute(polarized, "cell", up)
    high = lax.ppermute(polarized, "cell", [(t, s) for s, t in up])
    stacked = jnp.stack([low, polarized, high])
    summed = jnp.einsum("dik,dcekj->ceij", coulomb[0], stacked, preferred_element_type=F32)
    return summed.astype(BF16)[None]


def solution(mesh):
    n, cells = mesh.shape["energy"], mesh.shape["cell"]

    def on_device(retarded, sigma_lesser, sigma_greater, coulomb):
        norb = retarded.shape[-1]
        whole_tiles = n % QUARTERS == 0 and norb % LANES == 0 and norb % (n // QUARTERS * ROWS) == 0
        plan = fused if whole_tiles else thin
        return plan(n, cells, retarded, sigma_lesser, sigma_greater, coulomb)

    in_specs = (
        P("cell", None, "energy", None, None),
        P("cell", None, "energy", None, None),
        P("cell", None, "energy", None, None),
        P("cell", None, None, None),
    )
    out_specs = P("cell", None, "energy", None, None)
    return jax.shard_map(
        on_device, mesh=mesh, in_specs=in_specs, out_specs=out_specs, check_vma=False
    )
```
